256 devices in a mesh: vox: 64 (over y, z, core), comp: 4 (over x).
Axes of the slice: x: 4, y: 4, z: 8, core: 2. Of those that a mesh axis runs over, the one named last changes fastest.
Arguments:
- data: bfloat16 [2048, 65536], P('comp', 'vox'), may hold values from -108 to 108
- projection: bfloat16 [512, 2048], P(None, 'comp'), may hold values from -0.125 to 0.125
- initial: float32 [512, 512], P('comp'), may hold values from -0.25 to 0.25
Outputs:
- unmixing: float32 [512, 512], P('comp')
- sources: bfloat16 [512, 65536], P('comp', 'vox')
The draws below stay inside these ranges and needn't reach their ends.
All inputs are finite; a program needn't handle non-finite values.
Results may differ from the reference program's by a relative error of at most 0.008.
Values may be sent and summed in bfloat16 or wider, within the bound.
A program may use at most 64 MiB of HBM per device.

```python
import math
import jax
import jax.numpy as jnp
from jax import lax

P_SIZE = 2048
K = 512
ICA_ITERS = 2
WHITEN_STEPS = 3
DECOR_STEPS = 3
VOXELS = 65536


def draw_data(key, part):
    key_base = jax.random.fold_in(key, 11)
    key_rows = jax.random.fold_in(key, 12)
    key_cols = jax.random.fold_in(key, 13)
    base = jnp.clip(jax.random.normal(key_base, (P_SIZE, VOXELS), jnp.float32), -6.0, 6.0)
    rows = jnp.exp(jax.random.uniform(key_rows, (P_SIZE, 1), jnp.float32, math.log(0.5), math.log(2.0)))
    cols = jnp.exp(jax.random.uniform(key_cols, (1, VOXELS), jnp.float32, math.log(0.3), math.log(3.0)))
    place = jnp.arange(VOXELS, dtype=jnp.float32)[None, :] / (VOXELS - 1)
    trend = jnp.exp(math.log(3.0) * place)
    return (base * rows * cols * trend).astype(jnp.bfloat16)


def block_levels(stream_key, extent, shards, smallest, top_value):
    gain, own = 1.0, jax.random.fold_in(stream_key, 6)
    for position, parts in shards:
        steps = jnp.exp(jax.random.uniform(jax.random.fold_in(own, position), (parts,), jnp.float32, smallest / len(shards), top_value / len(shards)))
        gain = gain * jnp.repeat(steps, extent[position] // parts).reshape([-1 if axis == position else 1 for axis in range(len(extent))])
    return gain


def centred(own_key, extent, scale, limit, shards=(), kind=jnp.bfloat16):
    gain = block_levels(own_key, extent, shards, -0.22, 0.18) if shards else 1.0
    entries = jax.random.normal(own_key, extent, jnp.float32) * scale * gain
    return jnp.minimum(jnp.maximum(entries, -limit), limit).astype(kind)


def setup_inputs(seed: int = 0) -> dict:
    seeds = jax.random.split(jax.random.key(seed), 4)
    data = draw_data(jax.random.fold_in(seeds[3], 71), 0)
    projection = centred(seeds[1], (K, P_SIZE), P_SIZE ** -0.5, 0.125, ((1, 4),))
    initial = centred(seeds[2], (K, K), K ** -0.5, 0.25, ((0, 4),), jnp.float32)
    return {"data": data, "projection": projection, "initial": initial}


def mult(left, right):
    return jnp.dot(left, right, precision=lax.Precision.HIGHEST)

def whitening(covar):
    count = covar.shape[0]
    eye = jnp.eye(count, dtype=jnp.float32)
    cscale = jnp.sqrt(jnp.sum(covar * covar) + 1e-06)
    ymat = covar / cscale
    zmat = eye
    for step in range(WHITEN_STEPS):
        middle = 1.5 * eye - 0.5 * mult(zmat, ymat)
        ymat = mult(ymat, middle)
        zmat = mult(middle, zmat)
    return (zmat / jnp.sqrt(cscale)).astype(jnp.bfloat16)

def decorrelate(newer):
    gram = mult(newer, newer.T)
    newer = newer / jnp.sqrt(jnp.sqrt(jnp.sum(gram * gram) + 1e-06))
    for step in range(DECOR_STEPS):
        newer = 1.5 * newer - 0.5 * mult(mult(newer, newer.T), newer)
    return newer

def reference(data, projection, initial):
    reduced = jnp.dot(projection, data, preferred_element_type=jnp.float32).astype(jnp.bfloat16)
    covar = jnp.dot(reduced, reduced.T, preferred_element_type=jnp.float32) / VOXELS
    whiten = whitening(covar)
    whitened = jnp.dot(whiten, reduced, preferred_element_type=jnp.float32).astype(jnp.bfloat16)
    unmixing = initial
    for turn in range(ICA_ITERS):
        scores = jnp.dot(unmixing.astype(jnp.bfloat16), whitened, preferred_element_type=jnp.float32)
        bent = jnp.tanh(scores)
        pulled = jnp.dot(bent.astype(jnp.bfloat16), whitened.T, preferred_element_type=jnp.float32)
        slope = lax.optimization_barrier(jnp.sum(1.0 - bent * bent, axis=1))
        newer = pulled - slope[:, None] * unmixing
        unmixing = decorrelate(newer)
    sources = jnp.dot(unmixing.astype(jnp.bfloat16), whitened, preferred_element_type=jnp.float32).astype(jnp.bfloat16)
    return (unmixing, sources)
```

```python
import jax
import jax.numpy as jnp
from jax import lax
from jax.experimental import pallas as pl
from jax.experimental.pallas import tpu as pltpu
from jax.sharding import PartitionSpec as P

F32 = jnp.float32
BF16 = jnp.bfloat16
MESH = pl.DeviceIdType.MESH

K = 512
ROWS = 128
VOX = 1024
HALF = 512
VOXELS = 65536
ICA_ITERS = 2


def dot(a, b):
    return jnp.dot(a, b, preferred_element_type=F32)


def dot_nt(a, b):
    return lax.dot_general(a, b, (((1,), (1,)), ((), ())), preferred_element_type=F32)


def kernel(
    proj_hbm, data_hbm, init_hbm, un_ref, src_ref,
    proj, data, w, opp_s, right_s, left_s, own, ra, rb, red, wht, bent,
    pf, cs, cr, hf, hs, zr, ys, yr, full, fa, ba, bb, bc,
    ld_sem, ra_sem, rb_sem, ag_sem, xs_sem, s_sem, r_sem, zg_sem, xg_sem,
):
    v = lax.axis_index("vox")
    x = lax.axis_index("comp")
    c = lax.rem(v, 2)
    z = lax.rem(v // 2, 8)
    y = v // 16

    def dev(y_, z_, c_, x_):
        return ((y_ * 8 + z_) * 2 + c_, x_)

    def zoff(d):
        return lax.rem(z + d, 8)

    def xoff(d):
        return lax.rem(x + d, 4)

    ypeers = [y + 1 - 2 * lax.rem(y, 2), lax.rem(y + 2, 4), 3 - y]
    partner = dev(y, z, 1 - c, x)

    barrier = pltpu.get_barrier_semaphore()
    peers = [partner]
    peers += [dev(y, zoff(d), c, x) for d in range(1, 8)]
    peers += [dev(p, z, c, x) for p in ypeers]
    peers += [dev(y, z, c, xoff(d)) for d in range(1, 4)]
    for p in peers:
        pl.semaphore_signal(barrier, inc=1, device_id=p, device_id_type=MESH)

    loads = [
        pltpu.make_async_copy(proj_hbm, proj, ld_sem.at[0]),
        pltpu.make_async_copy(data_hbm, data, ld_sem.at[1]),
        pltpu.make_async_copy(init_hbm, w, ld_sem.at[2]),
    ]
    for ld in loads:
        ld.start()
    for ld in loads:
        ld.wait()

    def send(src, dst, ssem, rsem, to):
        cp = pltpu.make_async_remote_copy(
            src_ref=src, dst_ref=dst, send_sem=ssem, recv_sem=rsem,
            device_id=to, device_id_type=MESH,
        )
        cp.start()
        return cp

    def wait_for(ref, sem):
        pltpu.make_async_copy(ref, ref, sem).wait()

    def part(block):
        return dot(proj[pl.ds(pl.multiple_of(block * ROWS, ROWS), ROWS), :], data[...])

    xr, xo, xl = xoff(1), xoff(2), xoff(3)
    right, left = dev(y, z, c, xr), dev(y, z, c, xl)
    lo, hi = slice(0, HALF), slice(HALF, VOX)

    opp_s[...] = part(xo).astype(BF16)
    pl.semaphore_wait(barrier, len(peers))
    pend = []
    pend.append(send(opp_s.at[:, lo], ra.at[0], xs_sem.at[0], ra_sem.at[0], right))
    pend.append(send(opp_s.at[:, hi], ra.at[1], xs_sem.at[1], ra_sem.at[1], left))
    own[...] = part(xr)
    right_s[:, hi] = own[:, hi].astype(BF16)
    pend.append(send(right_s.at[:, hi], rb.at[0, :, hi], xs_sem.at[2], rb_sem.at[0], right))
    fa[0:ROWS, :] = own[:, lo]
    own[...] = part(xl)
    left_s[:, lo] = own[:, lo].astype(BF16)
    pend.append(send(left_s.at[:, lo], rb.at[1, :, lo], xs_sem.at[3], rb_sem.at[1], left))
    fa[ROWS:2 * ROWS, :] = own[:, hi]
    own[...] = part(x)
    wait_for(ra.at[0], ra_sem.at[0])
    right_s[:, lo] = (fa[0:ROWS, :] + ra[0].astype(F32)).astype(BF16)
    pend.append(send(right_s.at[:, lo], rb.at[0, :, lo], xs_sem.at[4], rb_sem.at[2], right))
    wait_for(ra.at[1], ra_sem.at[1])
    left_s[:, hi] = (fa[ROWS:2 * ROWS, :] + ra[1].astype(F32)).astype(BF16)
    pend.append(send(left_s.at[:, hi], rb.at[1, :, hi], xs_sem.at[5], rb_sem.at[3], left))
    wait_for(rb.at[0, :, hi], rb_sem.at[0])
    wait_for(rb.at[1, :, lo], rb_sem.at[1])
    wait_for(rb.at[0, :, lo], rb_sem.at[2])
    wait_for(rb.at[1, :, hi], rb_sem.at[3])

    def rows_of(block):
        return pl.ds(pl.multiple_of(block * ROWS, ROWS), ROWS)

    mine, rows_r, rows_l, rows_o = rows_of(x), rows_of(xr), rows_of(xl), rows_of(xo)
    red[mine, :] = (own[...] + rb[0].astype(F32) + rb[1].astype(F32)).astype(BF16)
    pend.append(send(red.at[mine, :], red.at[mine, :], xs_sem.at[6], ag_sem.at[0], right))
    pend.append(send(red.at[mine, :], red.at[mine, :], xs_sem.at[7], ag_sem.at[1], left))
    wait_for(red.at[rows_l, :], ag_sem.at[0])
    pend.append(send(red.at[rows_l, lo], red.at[rows_l, lo], xs_sem.at[8], ag_sem.at[2], right))
    wait_for(red.at[rows_r, :], ag_sem.at[1])
    pend.append(send(red.at[rows_r, hi], red.at[rows_r, hi], xs_sem.at[9], ag_sem.at[3], left))
    wait_for(red.at[rows_o, lo], ag_sem.at[2])
    wait_for(red.at[rows_o, hi], ag_sem.at[3])

    def piece_of(z_):
        return (
            pl.ds(pl.multiple_of(16 * (z_ // 2), 16), 16),
            pl.ds(pl.multiple_of(256 * lax.rem(z_, 2), 256), 256),
        )

    def half_of(x_, c_):
        return pl.ds(pl.multiple_of(x_ * ROWS + c_ * 64, 64), 64)

    def spot(x_, c_, z_):
        return (
            pl.ds(pl.multiple_of(x_ * ROWS + c_ * 64 + 16 * (z_ // 2), 16), 16),
            pl.ds(pl.multiple_of(256 * lax.rem(z_, 2), 256), 256),
        )

    def all_sum(s):
        cs[s] = pf[pl.ds(pl.multiple_of((1 - c) * 64, 64), 64), :].astype(BF16)
        send(cs.at[s], cr.at[s], s_sem.at[s, 0], r_sem.at[s, 0], partner)
        wait_for(cr.at[s], r_sem.at[s, 0])
        hf[...] = pf[pl.ds(pl.multiple_of(c * 64, 64), 64), :] + cr[s].astype(F32)
        hs[s] = hf[...].astype(BF16)
        for d in (4, 3, 5, 2, 6, 1, 7):
            to = zoff(d)
            a, b = piece_of(to)
            send(hs.at[s, a, b], zr.at[s, d - 1], s_sem.at[s, 1], r_sem.at[s, 1], dev(y, to, c, x))
        wait_for(zr.at[s], r_sem.at[s, 1])
        a, b = piece_of(z)
        acc = hf[a, b]
        for d in range(7):
            acc = acc + zr[s, d].astype(F32)
        ys[s] = acc.astype(BF16)
        for k in range(3):
            send(ys.at[s], yr.at[s, k], s_sem.at[s, 2], r_sem.at[s, 2], dev(ypeers[k], z, c, x))
        wait_for(yr.at[s], r_sem.at[s, 2])
        first = ys[s].astype(F32) + yr[s, 0].astype(F32)
        second = yr[s, 1].astype(F32) + yr[s, 2].astype(F32)
        a, b = spot(x, c, z)
        full[s, a, b] = (first + second).astype(BF16)
        for d in (4, 3, 5, 2, 6, 1, 7):
            send(full.at[s, a, b], full.at[s, a, b], s_sem.at[s, 3], zg_sem.at[s, d - 1], dev(y, zoff(d), c, x))

        def to_x(z_):
            a, b = spot(x, c, z_)
            for d in (2, 1, 3):
                send(full.at[s, a, b], full.at[s, a, b], s_sem.at[s, 4], xg_sem.at[s, d - 1], dev(y, z, c, xoff(d)))

        to_x(z)
        for d in (1, 7, 2, 6, 3, 5, 4):
            src = zoff(8 - d)
            a, b = spot(x, c, src)
            wait_for(full.at[s, a, b], zg_sem.at[s, d - 1])
            to_x(src)

        def to_partner(x_):
            h = half_of(x_, c)
            send(full.at[s, h, :], full.at[s, h, :], s_sem.at[s, 5], r_sem.at[s, 3], partner)

        to_partner(x)
        for d in (1, 3, 2):
            src = xoff(4 - d)
            wait_for(full.at[s, half_of(src, c), :], xg_sem.at[s, d - 1])
            to_partner(src)
        wait_for(full.at[s, 0:256, :], r_sem.at[s, 3])

    def sends_done(s):
        wait_for(cs.at[s], s_sem.at[s, 0])
        wait_for(zr.at[s], s_sem.at[s, 1])
        wait_for(yr.at[s], s_sem.at[s, 2])
        wait_for(zr.at[s], s_sem.at[s, 3])
        wait_for(full.at[s, 0:192, :], s_sem.at[s, 4])
        wait_for(full.at[s, 0:256, :], s_sem.at[s, 5])

    blocks = [slice(0, 256), slice(256, 512)]

    def square(ref):
        total = jnp.zeros((1, 1), F32)
        for n in blocks:
            total = total + jnp.sum(jnp.sum(ref[n, :] * ref[n, :], axis=0, keepdims=True), axis=1, keepdims=True)
        return total

    pf[...] = dot_nt(red[mine, :], red[...])
    all_sum(0)
    fa[...] = full[0].astype(F32) * (1.0 / VOXELS)
    cscale = jnp.sqrt(square(fa) + 1e-06)
    ba[...] = (fa[...] / cscale).astype(BF16)
    for n in blocks:
        fa[:, n] = 1.5 * ba[:, n].astype(F32) - 0.5 * dot(ba[...], ba[:, n])
    bb[...] = fa[...].astype(BF16)
    for n in blocks:
        bc[:, n] = (1.5 * fa[:, n] - 0.5 * dot(ba[...], bb[:, n])).astype(BF16)
    for n in blocks:
        fa[:, n] = 1.5 * fa[:, n] - 0.5 * dot(bb[...], bc[:, n])
    bb[...] = fa[...].astype(BF16)
    row = lax.broadcasted_iota(jnp.int32, (K, 256), 0)
    col = lax.broadcasted_iota(jnp.int32, (K, 256), 1)
    for i, n in enumerate(blocks):
        eye = jnp.where(row == col + 256 * i, 2.25, 0.0)
        fa[:, n] = (
            eye - 0.75 * (ba[:, n].astype(F32) + bc[:, n].astype(F32)) + 0.25 * dot(bc[...], ba[:, n])
        )
    ba[...] = fa[...].astype(BF16)
    for n in blocks:
        bc[:, n] = dot(ba[...], bb[:, n]).astype(BF16)
    inv = 1.0 / jnp.sqrt(cscale)
    for n in blocks:
        bb[:, n] = ((1.5 * fa[:, n] - 0.5 * dot(bc[...], ba[:, n])) * inv).astype(BF16)
    for j in range(4):
        n = slice(256 * j, 256 * j + 256)
        wht[:, n] = dot(bb[...], red[:, n]).astype(BF16)

    def turn(t, carry):
        s = t + 1
        weights = w[...]
        wb = weights.astype(BF16)
        slope = jnp.zeros((ROWS, 1), F32)
        for j in range(4):
            n = slice(256 * j, 256 * j + 256)
            th = jnp.tanh(dot(wb, wht[:, n]))
            bent[:, n] = th.astype(BF16)
            slope = slope + jnp.sum(1.0 - th * th, axis=1, keepdims=True)
        pf[...] = dot_nt(bent[...], wht[...]) - slope * weights
        all_sum(s)
        for n in blocks:
            fa[:, n] = dot_nt(full[s], full[s, n, :])
        norm = jnp.sqrt(square(fa) + 1e-06)
        scale = 1.0 / jnp.sqrt(norm)
        ba[...] = (fa[...] / norm).astype(BF16)
        for n in blocks:
            fa[:, n] = (1.5 * full[s, :, n].astype(F32) - 0.5 * dot(ba[...], full[s, :, n])) * scale
        bb[...] = fa[...].astype(BF16)
        for n in blocks:
            ba[:, n] = dot_nt(bb[...], bb[n, :]).astype(BF16)
        for n in blocks:
            fa[:, n] = 1.5 * fa[:, n] - 0.5 * dot(ba[...], bb[:, n])
        bb[...] = fa[...].astype(BF16)
        mixed = dot_nt(bb[mine, :], bb[...]).astype(BF16)
        w[...] = 1.5 * fa[mine, :] - 0.5 * dot(mixed, bb[...])
        return carry

    lax.fori_loop(0, ICA_ITERS, turn, 0)

    un_ref[...] = w[...]
    wb = w[...].astype(BF16)
    for j in range(4):
        n = slice(256 * j, 256 * j + 256)
        src_ref[:, n] = dot(wb, wht[:, n]).astype(BF16)

    for cp in pend:
        cp.wait_send()

    def drain(s, carry):
        sends_done(s)
        return carry

    lax.fori_loop(0, 1 + ICA_ITERS, drain, 0)


def shards(data, projection, initial):
    dma = pltpu.SemaphoreType.DMA
    stages = 1 + ICA_ITERS
    return tuple(pl.pallas_call(
        kernel,
        out_shape=(
            jax.ShapeDtypeStruct((ROWS, K), F32),
            jax.ShapeDtypeStruct((ROWS, VOX), BF16),
        ),
        in_specs=[pl.BlockSpec(memory_space=pl.ANY)] * 3,
        out_specs=[pl.BlockSpec(memory_space=pltpu.VMEM)] * 2,
        scratch_shapes=[
            pltpu.VMEM((K, 512), BF16),
            pltpu.VMEM((512, VOX), BF16),
            pltpu.VMEM((ROWS, K), F32),
            pltpu.VMEM((ROWS, VOX), BF16),
            pltpu.VMEM((ROWS, VOX), BF16),
            pltpu.VMEM((ROWS, VOX), BF16),
            pltpu.VMEM((ROWS, VOX), F32),
            pltpu.VMEM((2, ROWS, HALF), BF16),
            pltpu.VMEM((2, ROWS, VOX), BF16),
            pltpu.VMEM((K, VOX), BF16),
            pltpu.VMEM((K, VOX), BF16),
            pltpu.VMEM((ROWS, VOX), BF16),
            pltpu.VMEM((ROWS, K), F32),
            pltpu.VMEM((stages, 64, K), BF16),
            pltpu.VMEM((stages, 64, K), BF16),
            pltpu.VMEM((64, K), F32),
            pltpu.VMEM((stages, 64, K), BF16),
            pltpu.VMEM((stages, 7, 16, 256), BF16),
            pltpu.VMEM((stages, 16, 256), BF16),
            pltpu.VMEM((stages, 3, 16, 256), BF16),
            pltpu.VMEM((stages, K, K), BF16),
            pltpu.VMEM((K, K), F32),
            pltpu.VMEM((K, K), BF16),
            pltpu.VMEM((K, K), BF16),
            pltpu.VMEM((K, K), BF16),
            dma((3,)),
            dma((2,)),
            dma((4,)),
            dma((4,)),
            dma((10,)),
            dma((stages, 6)),
            dma((stages, 4)),
            dma((stages, 7)),
            dma((stages, 3)),
        ],
        compiler_params=pltpu.CompilerParams(collective_id=0, has_side_effects=True),
    )(projection, data, initial))


def solution(mesh):
    return jax.shard_map(
        shards,
        mesh=mesh,
        in_specs=(P("comp", "vox"), P(None, "comp"), P("comp", None)),
        out_specs=(P("comp", None), P("comp", "vox")),
        check_vma=False,
    )
```

```python
import jax
import jax.numpy as jnp
from jax import lax
from jax.experimental import pallas as pl
from jax.experimental.pallas import tpu as pltpu
from jax.sharding import PartitionSpec as P

F32 = jnp.float32
BF16 = jnp.bfloat16
MESH = pl.DeviceIdType.MESH

K = 512
ROWS = 128
VOX = 1024
HALF = 512
VOXELS = 65536
ICA_ITERS = 2


def dot(a, b):
    return jnp.dot(a, b, preferred_element_type=F32)


def dot_nt(a, b):
    return lax.dot_general(a, b, (((1,), (1,)), ((), ())), preferred_element_type=F32)


def kernel(
    proj_hbm, data_hbm, init_hbm, un_ref, src_ref,
    proj, data, w, opp_s, right_s, left_s, own, ra, rb, red, wht, bent,
    pf, cs, cr, hf, hs, yr, zs, zr, full, fa, ba, bb, bc,
    ld_sem, ra_sem, rb_sem, ag_sem, xs_sem, s_sem, r_sem, g_sem,
):
    v = lax.axis_index("vox")
    x = lax.axis_index("comp")
    c = lax.rem(v, 2)
    z = lax.rem(v // 2, 8)
    y = v // 16

    def dev(y_, z_, c_, x_):
        return ((y_ * 8 + z_) * 2 + c_, x_)

    def xoff(d):
        return lax.rem(x + d, 4)

    def yoff(d):
        return lax.rem(y + d, 4)

    def zxor(k):
        bits = [lax.rem(z, 2), lax.rem(z // 2, 2), z // 4]
        bits = [1 - b if (k >> i) % 2 else b for i, b in enumerate(bits)]
        return bits[0] + 2 * bits[1] + 4 * bits[2]

    partner = dev(y, z, 1 - c, x)

    barrier = pltpu.get_barrier_semaphore()
    peers = [partner]
    peers += [dev(y, zxor(k), c, x) for k in range(1, 8)]
    peers += [dev(yoff(dy), z, c, xoff(dx)) for dx in range(4) for dy in range(4) if dx or dy]
    for p in peers:
        pl.semaphore_signal(barrier, inc=1, device_id=p, device_id_type=MESH)

    loads = [
        pltpu.make_async_copy(proj_hbm, proj, ld_sem.at[0]),
        pltpu.make_async_copy(data_hbm, data, ld_sem.at[1]),
        pltpu.make_async_copy(init_hbm, w, ld_sem.at[2]),
    ]
    for ld in loads:
        ld.start()
    for ld in loads:
        ld.wait()

    def send(src, dst, ssem, rsem, to):
        cp = pltpu.make_async_remote_copy(
            src_ref=src, dst_ref=dst, send_sem=ssem, recv_sem=rsem,
            device_id=to, device_id_type=MESH,
        )
        cp.start()
        return cp

    def wait_for(ref, sem):
        pltpu.make_async_copy(ref, ref, sem).wait()

    def part(block):
        return dot(proj[pl.ds(pl.multiple_of(block * ROWS, ROWS), ROWS), :], data[...])

    xr, xo, xl = xoff(1), xoff(2), xoff(3)
    right, left = dev(y, z, c, xr), dev(y, z, c, xl)
    lo, hi = slice(0, HALF), slice(HALF, VOX)

    opp_s[...] = part(xo).astype(BF16)
    pl.semaphore_wait(barrier, len(peers))
    pend = []
    pend.append(send(opp_s.at[:, lo], ra.at[0], xs_sem.at[0], ra_sem.at[0], right))
    pend.append(send(opp_s.at[:, hi], ra.at[1], xs_sem.at[1], ra_sem.at[1], left))
    own[...] = part(xr)
    right_s[:, hi] = own[:, hi].astype(BF16)
    pend.append(send(right_s.at[:, hi], rb.at[0, :, hi], xs_sem.at[2], rb_sem.at[0], right))
    fa[0:ROWS, :] = own[:, lo]
    own[...] = part(xl)
    left_s[:, lo] = own[:, lo].astype(BF16)
    pend.append(send(left_s.at[:, lo], rb.at[1, :, lo], xs_sem.at[3], rb_sem.at[1], left))
    fa[ROWS:2 * ROWS, :] = own[:, hi]
    own[...] = part(x)
    wait_for(ra.at[0], ra_sem.at[0])
    right_s[:, lo] = (fa[0:ROWS, :] + ra[0].astype(F32)).astype(BF16)
    pend.append(send(right_s.at[:, lo], rb.at[0, :, lo], xs_sem.at[4], rb_sem.at[2], right))
    wait_for(ra.at[1], ra_sem.at[1])
    left_s[:, hi] = (fa[ROWS:2 * ROWS, :] + ra[1].astype(F32)).astype(BF16)
    pend.append(send(left_s.at[:, hi], rb.at[1, :, hi], xs_sem.at[5], rb_sem.at[3], left))
    wait_for(rb.at[0, :, hi], rb_sem.at[0])
    wait_for(rb.at[1, :, lo], rb_sem.at[1])
    wait_for(rb.at[0, :, lo], rb_sem.at[2])
    wait_for(rb.at[1, :, hi], rb_sem.at[3])

    def rows_of(block):
        return pl.ds(pl.multiple_of(block * ROWS, ROWS), ROWS)

    mine, rows_r, rows_l, rows_o = rows_of(x), rows_of(xr), rows_of(xl), rows_of(xo)
    red[mine, :] = (own[...] + rb[0].astype(F32) + rb[1].astype(F32)).astype(BF16)
    pend.append(send(red.at[mine, :], red.at[mine, :], xs_sem.at[6], ag_sem.at[0], right))
    pend.append(send(red.at[mine, :], red.at[mine, :], xs_sem.at[7], ag_sem.at[1], left))
    wait_for(red.at[rows_l, :], ag_sem.at[0])
    pend.append(send(red.at[rows_l, lo], red.at[rows_l, lo], xs_sem.at[8], ag_sem.at[2], right))
    wait_for(red.at[rows_r, :], ag_sem.at[1])
    pend.append(send(red.at[rows_r, hi], red.at[rows_r, hi], xs_sem.at[9], ag_sem.at[3], left))
    wait_for(red.at[rows_o, lo], ag_sem.at[2])
    wait_for(red.at[rows_o, hi], ag_sem.at[3])

    def half_of(x_, c_):
        return pl.ds(pl.multiple_of(x_ * ROWS + c_ * 64, 64), 64)

    def spot(x_, y_):
        return pl.ds(pl.multiple_of(x_ * ROWS + c * 64 + y_ * 16, 16), 16)

    plane = [(dx, dy) for dx in range(4) for dy in range(4) if dx or dy]
    plane.sort(key=lambda p: min(p[0], 4 - p[0]) + min(p[1], 4 - p[1]))

    def all_sum(s):
        cs[s] = pf[pl.ds(pl.multiple_of((1 - c) * 64, 64), 64), :].astype(BF16)
        send(cs.at[s], cr.at[s], s_sem.at[s, 0], r_sem.at[s, 0], partner)
        wait_for(cr.at[s], r_sem.at[s, 0])
        hf[...] = pf[pl.ds(pl.multiple_of(c * 64, 64), 64), :] + cr[s].astype(F32)
        hs[s] = hf[...].astype(BF16)
        for d in (2, 1, 3):
            to = yoff(d)
            rows = pl.ds(pl.multiple_of(to * 16, 16), 16)
            send(hs.at[s, rows, :], yr.at[s, d - 1], s_sem.at[s, 1], r_sem.at[s, 1], dev(to, z, c, x))
        wait_for(yr.at[s], r_sem.at[s, 1])
        acc = hf[pl.ds(pl.multiple_of(y * 16, 16), 16), :]
        for d in range(3):
            acc = acc + yr[s, d].astype(F32)
        zs[s] = acc.astype(BF16)
        for k in (4, 5, 3, 7, 2, 6, 1):
            send(zs.at[s], zr.at[s, k - 1], s_sem.at[s, 2], r_sem.at[s, 2], dev(y, zxor(k), c, x))
        wait_for(zr.at[s], r_sem.at[s, 2])
        terms = [zs[s].astype(F32)] + [zr[s, k].astype(F32) for k in range(7)]
        while len(terms) > 1:
            terms = [a + b for a, b in zip(terms[0::2], terms[1::2])]
        here = spot(x, y)
        full[s, here, :] = terms[0].astype(BF16)
        for dx, dy in reversed(plane):
            send(
                full.at[s, here, :], full.at[s, here, :], s_sem.at[s, 3], g_sem.at[s, dx * 4 + dy],
                dev(yoff(dy), z, c, xoff(dx)),
            )

        def to_partner(h):
            send(full.at[s, h, :], full.at[s, h, :], s_sem.at[s, 4], r_sem.at[s, 3], partner)

        to_partner(here)
        for dx, dy in plane:
            there = spot(xoff(4 - dx), yoff(4 - dy))
            wait_for(full.at[s, there, :], g_sem.at[s, dx * 4 + dy])
            to_partner(there)
        wait_for(full.at[s, 0:256, :], r_sem.at[s, 3])

    def sends_done(s):
        wait_for(cs.at[s], s_sem.at[s, 0])
        wait_for(yr.at[s], s_sem.at[s, 1])
        wait_for(zr.at[s], s_sem.at[s, 2])
        wait_for(full.at[s, 0:240, :], s_sem.at[s, 3])
        wait_for(full.at[s, 0:256, :], s_sem.at[s, 4])

    blocks = [slice(0, 256), slice(256, 512)]

    def square(ref):
        total = jnp.zeros((1, 1), F32)
        for n in blocks:
            total = total + jnp.sum(jnp.sum(ref[n, :] * ref[n, :], axis=0, keepdims=True), axis=1, keepdims=True)
        return total

    pf[...] = dot_nt(red[mine, :], red[...])
    all_sum(0)
    fa[...] = full[0].astype(F32) * (1.0 / VOXELS)
    cscale = jnp.sqrt(square(fa) + 1e-06)
    ba[...] = (fa[...] / cscale).astype(BF16)
    for n in blocks:
        fa[:, n] = 1.5 * ba[:, n].astype(F32) - 0.5 * dot(ba[...], ba[:, n])
    bb[...] = fa[...].astype(BF16)
    for n in blocks:
        bc[:, n] = (1.5 * fa[:, n] - 0.5 * dot(ba[...], bb[:, n])).astype(BF16)
    for n in blocks:
        fa[:, n] = 1.5 * fa[:, n] - 0.5 * dot(bb[...], bc[:, n])
    bb[...] = fa[...].astype(BF16)
    row = lax.broadcasted_iota(jnp.int32, (K, 256), 0)
    col = lax.broadcasted_iota(jnp.int32, (K, 256), 1)
    for i, n in enumerate(blocks):
        eye = jnp.where(row == col + 256 * i, 2.25, 0.0)
        fa[:, n] = (
            eye - 0.75 * (ba[:, n].astype(F32) + bc[:, n].astype(F32)) + 0.25 * dot(bc[...], ba[:, n])
        )
    ba[...] = fa[...].astype(BF16)
    for n in blocks:
        bc[:, n] = dot(ba[...], bb[:, n]).astype(BF16)
    inv = 1.0 / jnp.sqrt(cscale)
    for n in blocks:
        bb[:, n] = ((1.5 * fa[:, n] - 0.5 * dot(bc[...], ba[:, n])) * inv).astype(BF16)
    for j in range(4):
        n = slice(256 * j, 256 * j + 256)
        wht[:, n] = dot(bb[...], red[:, n]).astype(BF16)

    def turn(t, carry):
        s = t + 1
        weights = w[...]
        wb = weights.astype(BF16)
        slope = jnp.zeros((ROWS, 1), F32)
        for j in range(4):
            n = slice(256 * j, 256 * j + 256)
            th = jnp.tanh(dot(wb, wht[:, n]))
            bent[:, n] = th.astype(BF16)
            slope = slope + jnp.sum(1.0 - th * th, axis=1, keepdims=True)
        pf[...] = dot_nt(bent[...], wht[...]) - slope * weights
        all_sum(s)
        for n in blocks:
            fa[:, n] = dot_nt(full[s], full[s, n, :])
        norm = jnp.sqrt(square(fa) + 1e-06)
        scale = 1.0 / jnp.sqrt(norm)
        ba[...] = (fa[...] / norm).astype(BF16)
        for n in blocks:
            fa[:, n] = (1.5 * full[s, :, n].astype(F32) - 0.5 * dot(ba[...], full[s, :, n])) * scale
        bb[...] = fa[...].astype(BF16)
        for n in blocks:
            ba[:, n] = dot_nt(bb[...], bb[n, :]).astype(BF16)
        for n in blocks:
            fa[:, n] = 1.5 * fa[:, n] - 0.5 * dot(ba[...], bb[:, n])
        bb[...] = fa[...].astype(BF16)
        mixed = dot_nt(bb[mine, :], bb[...]).astype(BF16)
        w[...] = 1.5 * fa[mine, :] - 0.5 * dot(mixed, bb[...])
        return carry

    lax.fori_loop(0, ICA_ITERS, turn, 0)

    un_ref[...] = w[...]
    wb = w[...].astype(BF16)
    for j in range(4):
        n = slice(256 * j, 256 * j + 256)
        src_ref[:, n] = dot(wb, wht[:, n]).astype(BF16)

    for cp in pend:
        cp.wait_send()

    def drain(s, carry):
        sends_done(s)
        return carry

    lax.fori_loop(0, 1 + ICA_ITERS, drain, 0)


def shards(data, projection, initial):
    dma = pltpu.SemaphoreType.DMA
    stages = 1 + ICA_ITERS
    return tuple(pl.pallas_call(
        kernel,
        out_shape=(
            jax.ShapeDtypeStruct((ROWS, K), F32),
            jax.ShapeDtypeStruct((ROWS, VOX), BF16),
        ),
        in_specs=[pl.BlockSpec(memory_space=pl.ANY)] * 3,
        out_specs=[pl.BlockSpec(memory_space=pltpu.VMEM)] * 2,
        scratch_shapes=[
            pltpu.VMEM((K, 512), BF16),
            pltpu.VMEM((512, VOX), BF16),
            pltpu.VMEM((ROWS, K), F32),
            pltpu.VMEM((ROWS, VOX), BF16),
            pltpu.VMEM((ROWS, VOX), BF16),
            pltpu.VMEM((ROWS, VOX), BF16),
            pltpu.VMEM((ROWS, VOX), F32),
            pltpu.VMEM((2, ROWS, HALF), BF16),
            pltpu.VMEM((2, ROWS, VOX), BF16),
            pltpu.VMEM((K, VOX), BF16),
            pltpu.VMEM((K, VOX), BF16),
            pltpu.VMEM((ROWS, VOX), BF16),
            pltpu.VMEM((ROWS, K), F32),
            pltpu.VMEM((stages, 64, K), BF16),
            pltpu.VMEM((stages, 64, K), BF16),
            pltpu.VMEM((64, K), F32),
            pltpu.VMEM((stages, 64, K), BF16),
            pltpu.VMEM((stages, 3, 16, K), BF16),
            pltpu.VMEM((stages, 16, K), BF16),
            pltpu.VMEM((stages, 7, 16, K), BF16),
            pltpu.VMEM((stages, K, K), BF16),
            pltpu.VMEM((K, K), F32),
            pltpu.VMEM((K, K), BF16),
            pltpu.VMEM((K, K), BF16),
            pltpu.VMEM((K, K), BF16),
            dma((3,)),
            dma((2,)),
            dma((4,)),
            dma((4,)),
            dma((10,)),
            dma((stages, 5)),
            dma((stages, 4)),
            dma((stages, 16)),
        ],
        compiler_params=pltpu.CompilerParams(collective_id=0, has_side_effects=True),
    )(projection, data, initial))


def solution(mesh):
    return jax.shard_map(
        shards,
        mesh=mesh,
        in_specs=(P("comp", "vox"), P(None, "comp"), P("comp", None)),
        out_specs=(P("comp", None), P("comp", "vox")),
        check_vma=False,
    )
```
